32 devices in a mesh: slab: 2 (over y), tp: 4 (over x, core), band: 4 (over z).
Axes of the slice: x: 2, y: 2, z: 4, core: 2. Of those that a mesh axis runs over, the one named last changes fastest.
Arguments:
- tokens: bfloat16 [3072, 3072], P(('slab', 'band'), 'tp'), may hold values from -6 to 6
- w_qkv: bfloat16 [3072, 3, 3072], P('band', None, 'tp'), may hold values from -0.109375 to 0.109375
- w_out: bfloat16 [3072, 3072], P('tp'), may hold values from -0.109375 to 0.109375
- shift: float32 [3072], replicated, may hold values from -3 to 3
- scale: float32 [3072], replicated, may hold values from -0.9 to 0.9
- gate: float32 [3072], P('tp'), may hold values from 0.5 to 2
- q_gain: float32 [128], replicated, may hold values from 0.5 to 5.5
- k_gain: float32 [128], replicated, may hold values from 0.5 to 5.5
- tile_ids: int32 [24, 14], P(('slab', 'band')), may hold values from 0 to 23, as said below
- key_counts: int32 [24], P(('slab', 'band')), may hold values from 1 to 14, as said below
Outputs:
- update: bfloat16 [3072, 3072], P(('slab', 'band'), 'tp')
The draws below stay inside these ranges and needn't reach their ends.
Inputs may be any that keep to these rules, and one draw needn't show every extreme that they name: `tile_ids`: row q's first key_counts[q] entries are distinct tiles, the first being q itself, whose time index (tile // 12), row index ((tile // 3) % 4) and column index (tile % 3) each differ from q's by at most one; the remaining entries equal q. `key_counts`: 14 is reached in every draw.
All inputs are finite; a program needn't handle non-finite values.
Results may differ from the reference program's by a relative error of at most 0.014.
The reference program's roundings to bfloat16 on the way (of `normed`, `queries`, `keys`, `values`, `probs` and `attended`) count: a program that leaves them out, or rounds other values in their place, can miss the bound.
Values may be sent and summed in bfloat16 or wider, within the bound.
A program may use at most 128 MiB of HBM per device.

```python
import jax
import jax.numpy as jnp
from jax import lax

D = 3072
HD = 128
HEADS = 24
TC = 3
TILE = 128
WIN = 14
TT = 2
TR = 4
NTILES = 24
TOKENS = 3072


def pattern_tables(key):
    local_key = jax.random.fold_in(key, 71)
    first_key, second_key = jax.random.split(local_key)
    tile = jnp.arange(NTILES, dtype=jnp.int32)
    time_pos = tile // (TR * TC)
    row_pos = tile // TC % TR
    column_pos = tile % TC
    offset = jnp.arange(27, dtype=jnp.int32)
    time_near = time_pos[:, None] + offset[None, :] // 9 - 1
    row_near = row_pos[:, None] + offset[None, :] // 3 % 3 - 1
    column_near = column_pos[:, None] + offset[None, :] % 3 - 1
    inside = (time_near >= 0) & (time_near < TT) & (row_near >= 0) & (row_near < TR)
    inside = inside & (column_near >= 0) & (column_near < TC)
    near_id = (time_near * TR + row_near) * TC + column_near
    noise = jax.random.randint(first_key, (NTILES, 27), 0, 2 ** 20)
    priority = jnp.where(offset[None, :] == 13, 2 ** 30, 0) + inside.astype(jnp.int32) * 2 ** 26 + noise * 32 + offset[None, :]
    unused, order = lax.top_k(priority, WIN)
    chosen = jnp.take_along_axis(near_id, order, axis=1)
    upper = jnp.minimum(jnp.sum(inside.astype(jnp.int32), axis=1), WIN)
    number = jax.random.randint(second_key, (NTILES,), 1, upper + 1)
    number = jnp.where(tile == TC + 1, WIN, number).astype(jnp.int32)
    slot_ids = jnp.arange(WIN, dtype=jnp.int32)
    listed = jnp.where(slot_ids[None, :] < number[:, None], chosen, tile[:, None])
    return (listed.astype(jnp.int32), number)


def draw_tile_ids(key, part):
    return pattern_tables(key)[0]


def draw_key_counts(key, part):
    return pattern_tables(key)[1]


def gain_draw(key):
    return jax.random.uniform(key, (HD,), jnp.float32, 0.6, 1.6)


def draw_q_gain(key, part):
    return gain_draw(jax.random.fold_in(key, 11))


def draw_k_gain(key, part):
    return gain_draw(jax.random.fold_in(key, 13))


def block_scale(rng, dims, cuts, least, high):
    loudness = 1.0
    for axis_at, blocks in cuts:
        draws = jax.random.uniform(jax.random.fold_in(jax.random.fold_in(rng, 6), axis_at), (blocks,), jnp.float32, least / len(cuts), high / len(cuts))
        loudness = loudness * jnp.repeat(jnp.exp(draws), dims[axis_at] // blocks).reshape((-1,) + (1,) * (len(dims) - 1 - axis_at))
    return loudness


def normal_values(key, shape, scale, most, pieces=(), kind=jnp.bfloat16):
    entries = scale * jax.random.normal(key, shape, jnp.float32)
    if pieces:
        entries = entries * block_scale(key, shape, pieces, -0.22, 0.18)
    return jnp.clip(entries, -most, most).astype(kind)


def setup_inputs(seed: int = 0) -> dict:
    key_list = jax.random.split(jax.random.key(seed), 11)
    return {
        "tokens": normal_values(key_list[0], (TOKENS, D), 1.0, 6.0, ((0, 8), (1, 4))),
        "w_qkv": normal_values(key_list[1], (D, 3, D), D ** -0.5, 0.109375, ((0, 4), (2, 4))),
        "w_out": normal_values(key_list[2], (D, D), D ** -0.5, 0.109375, ((0, 4),)),
        "shift": normal_values(key_list[3], (D,), 0.5, 3.0, (), jnp.float32),
        "scale": normal_values(key_list[4], (D,), 0.3, 0.9, (), jnp.float32),
        "gate": jnp.clip(0.5 + 1.5 * jax.random.uniform(key_list[5], (D,), jnp.float32) ** block_scale(key_list[5], (D,), ((0, 4),), -0.2, 0.2), 0.5, 2.0),
        "q_gain": draw_q_gain(jax.random.fold_in(key_list[10], 71), 0),
        "k_gain": draw_k_gain(jax.random.fold_in(key_list[10], 71), 0),
        "tile_ids": draw_tile_ids(jax.random.fold_in(key_list[10], 71), 0),
        "key_counts": draw_key_counts(jax.random.fold_in(key_list[10], 71), 0),
    }


def head_norm(part, gain):
    squares = lax.optimization_barrier(jnp.mean(part * part, axis=-1, keepdims=True))
    return (part * lax.rsqrt(squares + 1e-06) * gain).astype(jnp.bfloat16)

def reference(tokens, w_qkv, w_out, shift, scale, gate, q_gain, k_gain, tile_ids, key_counts):
    floats = tokens.astype(jnp.float32)
    center = lax.optimization_barrier(jnp.mean(floats, axis=-1, keepdims=True))
    spread = lax.optimization_barrier(jnp.mean((floats - center) ** 2, axis=-1, keepdims=True))
    normed = ((floats - center) * lax.rsqrt(spread + 1e-06) * (1.0 + scale) + shift).astype(jnp.bfloat16)
    projected = jnp.dot(normed, w_qkv.reshape(D, 3 * D), preferred_element_type=jnp.float32)
    projected = projected.reshape(TOKENS, 3, HEADS, HD)
    queries = head_norm(projected[:, 0], q_gain)
    keys = head_norm(projected[:, 1], k_gain)
    values = projected[:, 2].astype(jnp.bfloat16)
    query_tiles = queries.reshape(NTILES, TILE, HEADS, HD)
    key_tiles = keys.reshape(NTILES, TILE, HEADS, HD)
    value_tiles = values.reshape(NTILES, TILE, HEADS, HD)
    inverse = 1.0 / HD ** 0.5

    def one_tile(items):
        listed, number, query = items
        near_keys = jnp.take(key_tiles, listed, axis=0).astype(jnp.float32)
        near_values = jnp.take(value_tiles, listed, axis=0).astype(jnp.float32)
        scores = jnp.einsum('qhd,wkhd->hqwk', query.astype(jnp.float32), near_keys) * inverse
        allowed = (jnp.arange(WIN) < number)[None, None, :, None]
        scores = jnp.where(allowed, scores, -1e+30)
        top = lax.optimization_barrier(jnp.max(scores, axis=(2, 3), keepdims=True))
        weights = jnp.exp(scores - top)
        probs = (weights / lax.optimization_barrier(jnp.sum(weights, axis=(2, 3), keepdims=True))).astype(jnp.bfloat16)
        result = jnp.einsum('hqwk,wkhd->qhd', probs.astype(jnp.float32), near_values)
        return result.astype(jnp.bfloat16)
    attended = lax.map(one_tile, (tile_ids, key_counts, query_tiles)).reshape(TOKENS, D)
    product = jnp.dot(attended, w_out, preferred_element_type=jnp.float32)
    return (gate * product).astype(jnp.bfloat16)
```

```python
import functools

import jax
import jax.numpy as jnp
from jax import lax
from jax.experimental import pallas as pl
from jax.experimental.pallas import tpu as pltpu
from jax.sharding import PartitionSpec as P

BF = jnp.bfloat16
F32 = jnp.float32


def proj_kernel(normalize, head_size, x_ref, scale_ref, shift_ref, w_ref, gain_ref, o_ref, normed):
    part = pl.program_id(1)

    @pl.when(part == 0)
    def _():
        floats = x_ref[...].astype(F32)
        center = jnp.mean(floats, axis=-1, keepdims=True)
        moved = floats - center
        spread = jnp.mean(moved * moved, axis=-1, keepdims=True)
        normed[...] = (
            moved * lax.rsqrt(spread + 1e-06) * (1.0 + scale_ref[...]) + shift_ref[...]
        ).astype(BF)

    product = jnp.dot(normed[...], w_ref[...], preferred_element_type=F32)

    def write(normed_part):
        for head in range(product.shape[1] // head_size):
            cols = slice(head * head_size, (head + 1) * head_size)
            piece = product[:, cols]
            if normed_part:
                squares = jnp.mean(piece * piece, axis=-1, keepdims=True)
                piece = piece * lax.rsqrt(squares + 1e-06) * gain_ref[...]
            o_ref[:, cols] = piece.astype(BF)

    if all(normalize):
        write(True)
    else:

        @pl.when(part == 0)
        def _():
            write(True)

        @pl.when(part != 0)
        def _():
            write(False)


def project(x, scale, shift, w, gain, normalize):
    rows, width = x.shape
    parts = len(normalize)
    cols = w.shape[1] // parts
    block = 256 if rows % 256 == 0 else rows
    return pl.pallas_call(
        functools.partial(proj_kernel, normalize, gain.shape[0]),
        grid=(rows // block, parts),
        in_specs=[
            pl.BlockSpec((block, width), lambda i, j: (i, 0)),
            pl.BlockSpec((1, width), lambda i, j: (0, 0)),
            pl.BlockSpec((1, width), lambda i, j: (0, 0)),
            pl.BlockSpec((width, cols), lambda i, j: (0, j)),
            pl.BlockSpec((1, gain.shape[0]), lambda i, j: (0, 0)),
        ],
        out_specs=pl.BlockSpec((block, cols), lambda i, j: (i, j)),
        out_shape=jax.ShapeDtypeStruct((rows, parts * cols), BF),
        scratch_shapes=[pltpu.VMEM((block, width), BF)],
        cost_estimate=pl.CostEstimate(
            flops=2 * rows * width * parts * cols,
            bytes_accessed=2 * (rows * width + width * parts * cols + rows * parts * cols),
            transcendentals=0,
        ),
        name="project",
    )(x, scale.reshape(1, -1), shift.reshape(1, -1), w, gain.reshape(1, -1))


def attend_kernel(head_size, place_ref, count_ref, q_ref, kv_ref, o_ref, sc):
    tile = pl.program_id(0)
    tile_len, feats = q_ref.shape
    heads = feats // head_size
    count = count_ref[tile]
    trips = (count + 1) // 2
    inverse = 1.0 / head_size**0.5
    lane = lax.broadcasted_iota(jnp.int32, (tile_len, 2 * tile_len), 1)

    def near(j, first, head):
        cols = slice(first + head * head_size, first + (head + 1) * head_size)
        one = kv_ref[place_ref[tile, 2 * j], :, cols]
        two = kv_ref[place_ref[tile, 2 * j + 1], :, cols]
        return jnp.concatenate([one, two], axis=0)

    def score(j, tops):
        limit = (count - 2 * j) * tile_len
        out = []
        for head in range(heads):
            query = q_ref[:, head * head_size : (head + 1) * head_size]
            scores = lax.dot_general(
                query, near(j, 0, head), (((1,), (1,)), ((), ())), preferred_element_type=F32
            )
            scores = jnp.where(lane < limit, scores * inverse, -1e30)
            sc[j, head] = scores
            out.append(jnp.maximum(tops[head], scores))
        return tuple(out)

    low = jnp.full((tile_len, 2 * tile_len), -1e30, F32)
    tops = lax.fori_loop(0, trips, score, (low,) * heads)
    tops = [jnp.max(top, axis=-1, keepdims=True) for top in tops]

    def weigh(j, sums):
        out = []
        for head in range(heads):
            weights = jnp.exp(sc[j, head] - tops[head])
            sc[j, head] = weights
            out.append(sums[head] + weights)
        return tuple(out)

    sums = lax.fori_loop(0, trips, weigh, (jnp.zeros((tile_len, 2 * tile_len), F32),) * heads)
    shares = [1.0 / jnp.sum(total, axis=-1, keepdims=True) for total in sums]

    def gather(j, totals):
        out = []
        for head in range(heads):
            probs = (sc[j, head] * shares[head]).astype(BF)
            out.append(
                totals[head] + jnp.dot(probs, near(j, feats, head), preferred_element_type=F32)
            )
        return tuple(out)

    totals = lax.fori_loop(0, trips, gather, (jnp.zeros((tile_len, head_size), F32),) * heads)
    for head in range(heads):
        o_ref[:, head * head_size : (head + 1) * head_size] = totals[head].astype(BF)


def attention(place, counts, queries, keys_values, head_size):
    tiles, slots = place.shape
    rows, feats = queries.shape
    tile_len = rows // tiles
    heads = feats // head_size
    many = keys_values.shape[0]
    if slots % 2:
        place = jnp.pad(place, ((0, 0), (0, 1)))
    return pl.pallas_call(
        functools.partial(attend_kernel, head_size),
        grid_spec=pltpu.PrefetchScalarGridSpec(
            num_scalar_prefetch=2,
            grid=(tiles,),
            in_specs=[
                pl.BlockSpec((tile_len, feats), lambda i, a, b: (i, 0)),
                pl.BlockSpec((many, tile_len, 2 * feats), lambda i, a, b: (0, 0, 0)),
            ],
            out_specs=pl.BlockSpec((tile_len, feats), lambda i, a, b: (i, 0)),
            scratch_shapes=[pltpu.VMEM(((slots + 1) // 2, heads, tile_len, 2 * tile_len), F32)],
        ),
        out_shape=jax.ShapeDtypeStruct((rows, feats), BF),
        cost_estimate=pl.CostEstimate(
            flops=4 * rows * slots * tile_len * feats,
            bytes_accessed=2 * (2 * rows * feats + many * tile_len * 2 * feats),
            transcendentals=rows * slots * tile_len * heads,
        ),
        name="attend",
    )(place, counts, queries, keys_values)


def shards(tokens, w_qkv, w_out, shift, scale, gate, q_gain, k_gain, tile_ids, key_counts):
    slabs, bands = lax.axis_size("slab"), lax.axis_size("band")
    slab_pos, band_pos = lax.axis_index("slab"), lax.axis_index("band")
    parity = slab_pos % 2
    tok_rows = tokens.shape[0]
    head_feats = w_out.shape[0]
    half = head_feats // 2
    head_size = q_gain.shape[0]
    tiles = key_counts.shape[0]
    tile_len = tok_rows // tiles
    swap = [(i, i ^ 1) for i in range(slabs)]

    other = lax.ppermute(tokens, "slab", swap)
    whole = lax.all_gather(jnp.concatenate([tokens, other], axis=0), "tp", axis=1, tiled=True)
    lists = jnp.concatenate([tile_ids, key_counts[:, None]], axis=1)
    lists = jnp.concatenate([lists, lax.ppermute(lists, "slab", swap)], axis=0)
    ids, counts = lists[:, :-1], lists[:, -1]

    mine = lax.dynamic_slice_in_dim(w_qkv, parity * half, half, axis=2)
    depth = mine.shape[0]
    w_kv = lax.all_gather(mine[:, 1:].reshape(depth, 2 * half), "band", axis=0, tiled=True)
    w_q = lax.all_gather(mine[:, 0].reshape(depth, half), "band", axis=0, tiled=True)

    joined = project(whole, scale, shift, w_kv, k_gain, (True, False))
    joined = joined.reshape(2, tiles, tile_len, 2 * half)
    if slabs > 2:
        first = jnp.where(parity == 0, joined[0], joined[1])
        second = jnp.where(parity == 0, joined[1], joined[0])
        up = [(i, i + 2) for i in range(slabs - 2)]
        below = lax.ppermute(second, "slab", up)
        above = lax.ppermute(first, "slab", [(b, a) for a, b in up])
        joined = jnp.concatenate([joined, below[None], above[None]], axis=0)
    groups = joined.shape[0]
    forward = [(i, i + 1) for i in range(bands - 1)]
    left = lax.ppermute(joined, "band", forward)
    right = lax.ppermute(joined, "band", [(b, a) for a, b in forward])
    queries = project(whole, scale, shift, w_q, q_gain, (True,))
    near = jnp.concatenate([left, joined, right], axis=0)
    near = near.reshape(3 * groups * tiles, tile_len, 2 * half)

    time_near = ids // (bands * tiles) - (slab_pos - parity)
    group = jnp.where(
        time_near < 0, 2, jnp.where(time_near > 1, 3, jnp.where(time_near == parity, 0, 1))
    )
    row_near = ids // tiles % bands - band_pos + 1
    place = (row_near * groups + group) * tiles + ids % tiles

    attended = attention(place, counts, queries, near, head_size)
    back = lax.ppermute(attended[tok_rows:], "slab", swap)
    ours = attended[:tok_rows]
    joint = jnp.where(
        parity == 0,
        jnp.concatenate([ours, back], axis=1),
        jnp.concatenate([back, ours], axis=1),
    )
    product = jnp.dot(joint, w_out, preferred_element_type=F32)
    shares = lax.psum_scatter(
        product.astype(BF), "tp", scatter_dimension=1, tiled=True
    ).astype(F32)
    return (gate * shares).astype(BF)


def solution(mesh):
    in_specs = (
        P(("slab", "band"), "tp"),
        P("band", None, "tp"),
        P("tp", None),
        P(),
        P(),
        P("tp"),
        P(),
        P(),
        P(("slab", "band"), None),
        P(("slab", "band")),
    )
    out_specs = P(("slab", "band"), "tp")
    return jax.shard_map(shards, mesh=mesh, in_specs=in_specs, out_specs=out_specs, check_vma=False)
```

```python
import functools

import jax
import jax.numpy as jnp
from jax import lax
from jax.experimental import pallas as pl
from jax.experimental.pallas import tpu as pltpu
from jax.sharding import PartitionSpec as P

BF = jnp.bfloat16
F32 = jnp.float32


def proj_kernel(normalize, head_size, x_ref, scale_ref, shift_ref, w_ref, gain_ref, o_ref, normed):
    part = pl.program_id(1)

    @pl.when(part == 0)
    def _():
        floats = jnp.concatenate([x_ref[0, i] for i in range(x_ref.shape[1])], axis=1).astype(F32)
        center = jnp.mean(floats, axis=-1, keepdims=True)
        moved = floats - center
        spread = jnp.mean(moved * moved, axis=-1, keepdims=True)
        normed[...] = (
            moved * lax.rsqrt(spread + 1e-06) * (1.0 + scale_ref[...]) + shift_ref[...]
        ).astype(BF)

    product = jnp.dot(normed[...], w_ref[...], preferred_element_type=F32)

    def write(normed_part):
        for head in range(product.shape[1] // head_size):
            cols = slice(head * head_size, (head + 1) * head_size)
            piece = product[:, cols]
            if normed_part:
                squares = jnp.mean(piece * piece, axis=-1, keepdims=True)
                piece = piece * lax.rsqrt(squares + 1e-06) * gain_ref[...]
            o_ref[:, cols] = piece.astype(BF)

    if all(normalize):
        write(True)
    else:

        @pl.when(part == 0)
        def _():
            write(True)

        @pl.when(part != 0)
        def _():
            write(False)


def project(x, scale, shift, w, first, gain, normalize):
    slabs, pieces, rows, width = x.shape
    width = pieces * width
    parts = len(normalize)
    cols = w.shape[1] // 3
    block = 192 if rows % 192 == 0 else rows
    many = rows // block
    return pl.pallas_call(
        functools.partial(proj_kernel, normalize, gain.shape[0]),
        grid=(slabs * many, parts),
        in_specs=[
            pl.BlockSpec((1, pieces, block, width // pieces), lambda i, j: (i // many, 0, i % many, 0)),
            pl.BlockSpec((1, width), lambda i, j: (0, 0)),
            pl.BlockSpec((1, width), lambda i, j: (0, 0)),
            pl.BlockSpec((width, cols), lambda i, j: (0, j + first)),
            pl.BlockSpec((1, gain.shape[0]), lambda i, j: (0, 0)),
        ],
        out_specs=pl.BlockSpec((block, cols), lambda i, j: (i, j)),
        out_shape=jax.ShapeDtypeStruct((slabs * rows, parts * cols), BF),
        scratch_shapes=[pltpu.VMEM((block, width), BF)],
        cost_estimate=pl.CostEstimate(
            flops=2 * slabs * rows * width * parts * cols,
            bytes_accessed=2 * (slabs * rows * width + width * parts * cols),
            transcendentals=0,
        ),
        name="project",
    )(x, scale.reshape(1, -1), shift.reshape(1, -1), w, gain.reshape(1, -1))


def gather_kernel(tps, chunks, tok_in, w_in, tok, w_all, relay, transit, z_send, z_recv, p_send,
                  p_recv, up_send, fwd_send, core_send, w_recv, t_recv, local):
    s, t, b = lax.axis_index("slab"), lax.axis_index("tp"), lax.axis_index("band")
    e, c = s % 2, t % 2
    base = s - e
    couples = tps // 2
    couple = t // 2

    def dev(slab, tp, band):
        return {"slab": slab, "tp": tp, "band": band}

    barrier = pltpu.get_barrier_semaphore()
    peers = [dev(s, t, (b + i) % 4) for i in range(1, 4)]
    for i in range(2):
        for j in range(tps):
            if i or j:
                peers.append(dev(base + (e + i) % 2, (t + j) % tps, b))
    for peer in peers:
        pl.semaphore_signal(barrier, inc=1, device_id=peer, device_id_type=pl.DeviceIdType.MESH)
    pl.semaphore_wait(barrier, len(peers))

    def remote(src, dst, send, recv, peer):
        return pltpu.make_async_remote_copy(
            src, dst, send, recv, device_id=peer, device_id_type=pl.DeviceIdType.MESH
        )

    q_own = b % 2
    planes = [b // 2, 2 + b // 2]
    legs = [
        remote(tok_in, relay.at[q_own], z_send.at[i], z_recv.at[q_own], dev(s, t, planes[i]))
        for i in range(2)
    ]
    for i in range(2):

        @pl.when(planes[i] != b)
        def _(leg=legs[i]):
            leg.start()

    u = jnp.where(c == 1, b, 3 - b)
    step = jnp.where(c == 1, 1, -1)
    ahead, behind = jnp.clip(b + step, 0, 3), jnp.clip(b - step, 0, 3)

    def slot(at):
        return jnp.where(c == 1, at, 3 - at)

    depth = w_in.shape[0] // chunks
    rows = [pl.ds(k * depth, depth) for k in range(chunks)]
    partner = dev(s, t + 1 - 2 * c, b)

    def own(k, where):
        if where == 0:
            return remote(w_in.at[rows[k]], transit.at[rows[k]], up_send.at[k], t_recv.at[k], dev(s, t, ahead))
        peer = dev(s, t, behind if where == 3 else ahead)
        return remote(w_in.at[rows[k]], w_all.at[b, rows[k]], up_send.at[k], w_recv.at[b, k], peer)

    def forward(src, k, at, n):
        place = slot(at)
        return remote(src, w_all.at[place, rows[k]], fwd_send.at[n, k], w_recv.at[place, k], dev(s, t, ahead))

    def across(src, k, at):
        place = slot(at)
        return remote(src, w_all.at[place, rows[k]], core_send.at[at, k], w_recv.at[place, k], partner)

    def arrived(k, at):
        place = slot(at)
        return remote(w_in.at[rows[k]], w_all.at[place, rows[k]], up_send.at[k], w_recv.at[place, k], partner)

    keep = pltpu.make_async_copy(w_in, w_all.at[b], local.at[2])
    for where in range(4):

        @pl.when(u == where)
        def _(where=where):
            for k in range(chunks):
                own(k, where).start()
            if where >= 2:
                keep.start()
                for k in range(chunks):
                    across(w_in.at[rows[k]], k, where).start()

    def spread(src, q):
        copies = []
        for i in range(2):
            for j in range(couples):
                peer = dev(base + (e + i) % 2, 2 * ((couple + j) % couples) + q, b)
                copies.append(remote(
                    src, tok.at[e, t], p_send.at[q, i * couples + j], p_recv.at[e, t], peer
                ))
        return copies, pltpu.make_async_copy(src, tok.at[e, t], local.at[q])

    for q in range(2):
        source = 2 * (b % 2) + q

        def send(src, q=q):
            copies, here = spread(src, q)
            for copy in copies[1:]:
                copy.start()

            @pl.when(c == q)
            def _():
                here.start()

            @pl.when(c != q)
            def _():
                copies[0].start()

        @pl.when(source == b)
        def _(send=send):
            send(tok_in)

        @pl.when(source != b)
        def _(send=send, q=q):
            remote(tok_in, relay.at[q], z_send.at[0], z_recv.at[q], partner).wait_recv()
            send(relay.at[q])

    @pl.when(u == 1)
    def _():
        for k in range(chunks):
            remote(w_in.at[rows[k]], transit.at[rows[k]], up_send.at[k], t_recv.at[k], partner).wait_recv()
            forward(transit.at[rows[k]], k, 0, 0).start()

    @pl.when(u == 2)
    def _():
        for n, at in enumerate((1, 0)):
            for k in range(chunks):
                arrived(k, at).wait_recv()
                src = w_all.at[slot(at), rows[k]]
                forward(src, k, at, n).start()
                across(src, k, at).start()
        for k in range(chunks):
            arrived(k, 3).wait_recv()
            across(w_all.at[slot(3), rows[k]], k, 3).start()

    @pl.when(u == 3)
    def _():
        for at in (2, 1, 0):
            for k in range(chunks):
                arrived(k, at).wait_recv()
                across(w_all.at[slot(at), rows[k]], k, at).start()

    @pl.when(u < 2)
    def _():
        for at in range(4):
            for k in range(chunks):
                arrived(k, at).wait_recv()

    for where in range(4):

        @pl.when(u == where)
        def _(where=where):
            for k in range(chunks):
                own(k, where).wait_send()
                if where == 1:
                    forward(transit.at[rows[k]], k, 0, 0).wait_send()
                if where == 2:
                    for n, at in enumerate((1, 0)):
                        forward(w_all.at[slot(at), rows[k]], k, at, n).wait_send()
                if where >= 2:
                    for at in range(4):
                        across(w_in.at[rows[k]], k, at).wait_send()
            if where >= 2:
                keep.wait()

    for i in range(2):

        @pl.when(planes[i] != b)
        def _(leg=legs[i]):
            leg.wait_send()

    for q in range(2):
        copies, here = spread(tok_in, q)
        for copy in copies[1:]:
            copy.wait_send()

        @pl.when(c == q)
        def _(here=here):
            here.wait()

        @pl.when(c != q)
        def _(copy=copies[0]):
            copy.wait_send()

    for i in range(2):
        for j in range(tps):
            if i or j:
                from_e, from_t = (e + i) % 2, (t + j) % tps
                remote(
                    tok_in, tok.at[from_e, from_t], p_send.at[0, 0], p_recv.at[from_e, from_t], partner
                ).wait_recv()


def gather_all(tokens, w, tps):
    chunks = 2
    dma = pltpu.SemaphoreType.DMA
    vmem = pl.BlockSpec(memory_space=pltpu.VMEM)
    return pl.pallas_call(
        functools.partial(gather_kernel, tps, chunks),
        out_shape=(
            jax.ShapeDtypeStruct((2, tps) + tokens.shape, BF),
            jax.ShapeDtypeStruct((4,) + w.shape, BF),
        ),
        in_specs=[vmem, vmem],
        out_specs=(vmem, vmem),
        scratch_shapes=[
            pltpu.VMEM((2,) + tokens.shape, BF),
            pltpu.VMEM(w.shape, BF),
            dma((2,)), dma((2,)), dma((2, tps)), dma((2, tps)),
            dma((chunks,)), dma((2, chunks)), dma((4, chunks)), dma((4, chunks)),
            dma((chunks,)), dma((3,)),
        ],
        compiler_params=pltpu.CompilerParams(collective_id=0, has_side_effects=True),
        name="gather_all",
    )(tokens, w)


def attend_kernel(head_size, place_ref, count_ref, q_ref, kv_ref, o_ref, sc):
    tile = pl.program_id(0)
    tile_len, feats = q_ref.shape
    heads = feats // head_size
    count = count_ref[tile]
    trips = (count + 1) // 2
    inverse = 1.0 / head_size**0.5
    lane = lax.broadcasted_iota(jnp.int32, (tile_len, 2 * tile_len), 1)

    def near(j, first, head):
        cols = slice(first + head * head_size, first + (head + 1) * head_size)
        one = kv_ref[place_ref[tile, 2 * j], :, cols]
        two = kv_ref[place_ref[tile, 2 * j + 1], :, cols]
        return jnp.concatenate([one, two], axis=0)

    def score(j, tops):
        limit = (count - 2 * j) * tile_len
        out = []
        for head in range(heads):
            query = q_ref[:, head * head_size : (head + 1) * head_size]
            scores = lax.dot_general(
                query, near(j, 0, head), (((1,), (1,)), ((), ())), preferred_element_type=F32
            )
            scores = jnp.where(lane < limit, scores * inverse, -1e30)
            sc[j, head] = scores
            out.append(jnp.maximum(tops[head], scores))
        return tuple(out)

    low = jnp.full((tile_len, 2 * tile_len), -1e30, F32)
    tops = lax.fori_loop(0, trips, score, (low,) * heads)
    tops = [jnp.max(top, axis=-1, keepdims=True) for top in tops]

    def weigh(j, sums):
        out = []
        for head in range(heads):
            weights = jnp.exp(sc[j, head] - tops[head])
            sc[j, head] = weights
            out.append(sums[head] + weights)
        return tuple(out)

    sums = lax.fori_loop(0, trips, weigh, (jnp.zeros((tile_len, 2 * tile_len), F32),) * heads)
    shares = [1.0 / jnp.sum(total, axis=-1, keepdims=True) for total in sums]

    def gather(j, totals):
        out = []
        for head in range(heads):
            probs = (sc[j, head] * shares[head]).astype(BF)
            out.append(
                totals[head] + jnp.dot(probs, near(j, feats, head), preferred_element_type=F32)
            )
        return tuple(out)

    totals = lax.fori_loop(0, trips, gather, (jnp.zeros((tile_len, head_size), F32),) * heads)
    for head in range(heads):
        o_ref[:, head * head_size : (head + 1) * head_size] = totals[head].astype(BF)


def attention(place, counts, queries, keys_values, head_size):
    tiles, slots = place.shape
    rows, feats = queries.shape
    tile_len = rows // tiles
    heads = feats // head_size
    many = keys_values.shape[0]
    if slots % 2:
        place = jnp.pad(place, ((0, 0), (0, 1)))
    return pl.pallas_call(
        functools.partial(attend_kernel, head_size),
        grid_spec=pltpu.PrefetchScalarGridSpec(
            num_scalar_prefetch=2,
            grid=(tiles,),
            in_specs=[
                pl.BlockSpec((tile_len, feats), lambda i, a, b: (i, 0)),
                pl.BlockSpec((many, tile_len, 2 * feats), lambda i, a, b: (0, 0, 0)),
            ],
            out_specs=pl.BlockSpec((tile_len, feats), lambda i, a, b: (i, 0)),
            scratch_shapes=[pltpu.VMEM(((slots + 1) // 2, heads, tile_len, 2 * tile_len), F32)],
        ),
        out_shape=jax.ShapeDtypeStruct((rows, feats), BF),
        cost_estimate=pl.CostEstimate(
            flops=4 * rows * slots * tile_len * feats,
            bytes_accessed=2 * (2 * rows * feats + many * tile_len * 2 * feats),
            transcendentals=rows * slots * tile_len * heads,
        ),
        name="attend",
    )(place, counts, queries, keys_values)


def shards(tokens, w_qkv, w_out, shift, scale, gate, q_gain, k_gain, tile_ids, key_counts):
    slabs, bands = lax.axis_size("slab"), lax.axis_size("band")
    slab_pos, band_pos = lax.axis_index("slab"), lax.axis_index("band")
    parity = slab_pos % 2
    tok_rows = tokens.shape[0]
    head_feats = w_out.shape[0]
    half = head_feats // 2
    head_size = q_gain.shape[0]
    tiles = key_counts.shape[0]
    tile_len = tok_rows // tiles
    tps = lax.axis_size("tp")
    tp_pos = lax.axis_index("tp")
    swap = [(i, i ^ 1) for i in range(slabs)]

    band_here = 2 * (band_pos % 2) + tp_pos % 2

    def flat(couple, core, side, low):
        return (2 * couple + core) * bands + 2 * side + low

    every = [
        (couple, i // 4, i // 2 % 2, i % 2) for couple in range(tps // 2) for i in range(8)
    ]
    outward = [(flat(n, c, h, l), flat(n, h, l, c)) for n, c, h, l in every]
    size = tps * bands
    outward_swap = [
        (i * size + source, (i ^ 1) * size + target)
        for i in range(slabs)
        for source, target in outward
    ]
    forward = [
        (flat(n, i % 2, h, i // 2), flat(n, (i + 1) % 2, h, (i + 1) // 2))
        for n in range(tps // 2)
        for h in range(2)
        for i in range(3)
    ]

    def both(ours, theirs, axis):
        return jnp.where(
            parity == 0,
            jnp.concatenate([ours, theirs], axis=axis),
            jnp.concatenate([theirs, ours], axis=axis),
        )

    mine = lax.dynamic_slice_in_dim(w_qkv, parity * half, half, axis=2)
    depth = mine.shape[0]
    whole, weights = gather_all(tokens, mine.reshape(depth, 3 * half), tps)
    weights = weights.reshape(4 * depth, 3 * half)

    lists = jnp.concatenate([tile_ids, key_counts[:, None]], axis=1)
    ours = lax.ppermute(lists, ("tp", "band"), [(b, a) for a, b in outward])
    theirs = lax.ppermute(
        lists, ("slab", "tp", "band"), [(b, a) for a, b in outward_swap]
    )
    lists = both(ours, theirs, 0)
    ids, counts = lists[:, :-1], lists[:, -1]

    joined = project(whole, scale, shift, weights, 1, k_gain, (True, False))
    joined = joined.reshape(2, tiles, tile_len, 2 * half)
    if slabs > 2:
        up = [(i, i + 2) for i in range(slabs - 2)]
        below = lax.ppermute(joined[1], "slab", up)
        above = lax.ppermute(joined[0], "slab", [(b, a) for a, b in up])
        joined = jnp.concatenate([joined, below[None], above[None]], axis=0)
    groups = joined.shape[0]
    left = lax.ppermute(joined, ("tp", "band"), forward)
    right = lax.ppermute(joined, ("tp", "band"), [(b, a) for a, b in forward])
    queries = project(whole, scale, shift, weights, 0, q_gain, (True,))
    near = jnp.concatenate([left, joined, right], axis=0)
    near = near.reshape(3 * groups * tiles, tile_len, 2 * half)

    time_near = ids // (bands * tiles) - (slab_pos - parity)
    group = jnp.where(time_near < 0, 2, jnp.where(time_near > 1, 3, time_near))
    row_near = ids // tiles % bands - band_here + 1
    place = (row_near * groups + group) * tiles + ids % tiles

    attended = attention(place, counts, queries, near, head_size)
    halves = attended.reshape(2, tok_rows, half)
    ours = jnp.where(parity == 0, halves[0], halves[1])
    theirs = jnp.where(parity == 0, halves[1], halves[0])
    ours = lax.ppermute(ours, ("tp", "band"), outward)
    theirs = lax.ppermute(theirs, ("slab", "tp", "band"), outward_swap)
    joint = both(ours, theirs, 1)
    product = jnp.dot(joint, w_out, preferred_element_type=F32)
    shares = lax.psum_scatter(
        product.astype(BF), "tp", scatter_dimension=1, tiled=True
    ).astype(F32)
    return (gate * shares).astype(BF)


def solution(mesh):
    in_specs = (
        P(("slab", "band"), "tp"),
        P("band", None, "tp"),
        P("tp", None),
        P(),
        P(),
        P("tp"),
        P(),
        P(),
        P(("slab", "band"), None),
        P(("slab", "band")),
    )
    out_specs = P(("slab", "band"), "tp")
    return jax.shard_map(shards, mesh=mesh, in_specs=in_specs, out_specs=out_specs, check_vma=False)
```

```python
import functools

import jax
import jax.numpy as jnp
from jax import lax
from jax.experimental import pallas as pl
from jax.experimental.pallas import tpu as pltpu
from jax.sharding import PartitionSpec as P

BF = jnp.bfloat16
F32 = jnp.float32


def proj_kernel(normalize, head_size, x_ref, scale_ref, shift_ref, w_ref, gain_ref, o_ref, normed):
    part = pl.program_id(1)

    @pl.when(part == 0)
    def _():
        floats = jnp.concatenate([x_ref[0, i] for i in range(x_ref.shape[1])], axis=1).astype(F32)
        center = jnp.mean(floats, axis=-1, keepdims=True)
        moved = floats - center
        spread = jnp.mean(moved * moved, axis=-1, keepdims=True)
        normed[...] = (
            moved * lax.rsqrt(spread + 1e-06) * (1.0 + scale_ref[...]) + shift_ref[...]
        ).astype(BF)

    weights = w_ref[...].reshape(normed.shape[1], w_ref.shape[3])
    product = jnp.dot(normed[...], weights, preferred_element_type=F32)

    def write(normed_part):
        for head in range(product.shape[1] // head_size):
            cols = slice(head * head_size, (head + 1) * head_size)
            piece = product[:, cols]
            if normed_part:
                squares = jnp.mean(piece * piece, axis=-1, keepdims=True)
                piece = piece * lax.rsqrt(squares + 1e-06) * gain_ref[...]
            o_ref[:, cols] = piece.astype(BF)

    if all(normalize):
        write(True)
    else:

        @pl.when(part == 0)
        def _():
            write(True)

        @pl.when(part != 0)
        def _():
            write(False)


def project(x, scale, shift, w, first, gain, normalize):
    slabs, pieces, rows, width = x.shape
    width = pieces * width
    parts = len(normalize)
    cols = w.shape[3]
    block = 192 if rows % 192 == 0 else rows
    many = rows // block
    return pl.pallas_call(
        functools.partial(proj_kernel, normalize, gain.shape[0]),
        grid=(slabs * many, parts),
        in_specs=[
            pl.BlockSpec((1, pieces, block, width // pieces), lambda i, j: (i // many, 0, i % many, 0)),
            pl.BlockSpec((1, width), lambda i, j: (0, 0)),
            pl.BlockSpec((1, width), lambda i, j: (0, 0)),
            pl.BlockSpec((w.shape[0], 1) + w.shape[2:], lambda i, j: (0, j + first, 0, 0)),
            pl.BlockSpec((1, gain.shape[0]), lambda i, j: (0, 0)),
        ],
        out_specs=pl.BlockSpec((block, cols), lambda i, j: (i, j)),
        out_shape=jax.ShapeDtypeStruct((slabs * rows, parts * cols), BF),
        scratch_shapes=[pltpu.VMEM((block, width), BF)],
        cost_estimate=pl.CostEstimate(
            flops=2 * slabs * rows * width * parts * cols,
            bytes_accessed=2 * (slabs * rows * width + width * parts * cols),
            transcendentals=0,
        ),
        name="project",
    )(x, scale.reshape(1, -1), shift.reshape(1, -1), w, gain.reshape(1, -1))


def gather_kernel(tps, chunks, tok_in, w_in, tok, w_all, relay, transit, z_send, z_recv, p_send,
                  p_recv, up_send, fwd_send, core_send, w_recv, t_recv, local):
    s, t, b = lax.axis_index("slab"), lax.axis_index("tp"), lax.axis_index("band")
    e, c = s % 2, t % 2
    base = s - e
    couples = tps // 2
    couple = t // 2

    def dev(slab, tp, band):
        return {"slab": slab, "tp": tp, "band": band}

    barrier = pltpu.get_barrier_semaphore()
    peers = [dev(s, t, (b + i) % 4) for i in range(1, 4)]
    for i in range(2):
        for j in range(tps):
            if i or j:
                peers.append(dev(base + (e + i) % 2, (t + j) % tps, b))
    for peer in peers:
        pl.semaphore_signal(barrier, inc=1, device_id=peer, device_id_type=pl.DeviceIdType.MESH)
    pl.semaphore_wait(barrier, len(peers))

    def remote(src, dst, send, recv, peer):
        return pltpu.make_async_remote_copy(
            src, dst, send, recv, device_id=peer, device_id_type=pl.DeviceIdType.MESH
        )

    q_own = b % 2
    planes = [b // 2, 2 + b // 2]
    legs = [
        remote(tok_in, relay.at[q_own], z_send.at[i], z_recv.at[q_own], dev(s, t, planes[i]))
        for i in range(2)
    ]
    for i in range(2):

        @pl.when(planes[i] != b)
        def _(leg=legs[i]):
            leg.start()

    u = jnp.where(c == 1, b, 3 - b)
    step = jnp.where(c == 1, 1, -1)
    ahead, behind = jnp.clip(b + step, 0, 3), jnp.clip(b - step, 0, 3)

    def slot(at):
        return jnp.where(c == 1, at, 3 - at)

    rows = list(range(chunks))
    partner = dev(s, t + 1 - 2 * c, b)

    def own(k, where):
        if where == 0:
            return remote(w_in.at[rows[k]], transit.at[rows[k]], up_send.at[k], t_recv.at[k], dev(s, t, ahead))
        peer = dev(s, t, behind if where == 3 else ahead)
        return remote(w_in.at[rows[k]], w_all.at[b, rows[k]], up_send.at[k], w_recv.at[b, k], peer)

    def forward(src, k, at, n):
        place = slot(at)
        return remote(src, w_all.at[place, rows[k]], fwd_send.at[n, k], w_recv.at[place, k], dev(s, t, ahead))

    def across(src, k, at):
        place = slot(at)
        return remote(src, w_all.at[place, rows[k]], core_send.at[at, k], w_recv.at[place, k], partner)

    def arrived(k, at):
        place = slot(at)
        return remote(w_in.at[rows[k]], w_all.at[place, rows[k]], up_send.at[k], w_recv.at[place, k], partner)

    keep = pltpu.make_async_copy(w_in, w_all.at[b], local.at[2])
    for where in range(4):

        @pl.when(u == where)
        def _(where=where):
            for k in range(chunks):
                own(k, where).start()
            if where >= 2:
                keep.start()
                for k in range(chunks):
                    across(w_in.at[rows[k]], k, where).start()

    def spread(src, q):
        copies = []
        for i in range(2):
            for j in range(couples):
                peer = dev(base + (e + i) % 2, 2 * ((couple + j) % couples) + q, b)
                copies.append(remote(
                    src, tok.at[e, t], p_send.at[q, i * couples + j], p_recv.at[e, t], peer
                ))
        return copies, pltpu.make_async_copy(src, tok.at[e, t], local.at[q])

    for q in range(2):
        source = 2 * (b % 2) + q

        def send(src, q=q):
            copies, here = spread(src, q)
            for copy in copies[1:]:
                copy.start()

            @pl.when(c == q)
            def _():
                here.start()

            @pl.when(c != q)
            def _():
                copies[0].start()

        @pl.when(source == b)
        def _(send=send):
            send(tok_in)

        @pl.when(source != b)
        def _(send=send, q=q):
            remote(tok_in, relay.at[q], z_send.at[0], z_recv.at[q], partner).wait_recv()
            send(relay.at[q])

    @pl.when(u == 1)
    def _():
        for k in range(chunks):
            remote(w_in.at[rows[k]], transit.at[rows[k]], up_send.at[k], t_recv.at[k], partner).wait_recv()
            forward(transit.at[rows[k]], k, 0, 0).start()

    @pl.when(u == 2)
    def _():
        for n, at in enumerate((1, 0)):
            for k in range(chunks):
                arrived(k, at).wait_recv()
                src = w_all.at[slot(at), rows[k]]
                forward(src, k, at, n).start()
                across(src, k, at).start()
        for k in range(chunks):
            arrived(k, 3).wait_recv()
            across(w_all.at[slot(3), rows[k]], k, 3).start()

    @pl.when(u == 3)
    def _():
        for at in (2, 1, 0):
            for k in range(chunks):
                arrived(k, at).wait_recv()
                across(w_all.at[slot(at), rows[k]], k, at).start()

    @pl.when(u < 2)
    def _():
        for at in range(4):
            for k in range(chunks):
                arrived(k, at).wait_recv()

    for where in range(4):

        @pl.when(u == where)
        def _(where=where):
            for k in range(chunks):
                own(k, where).wait_send()
                if where == 1:
                    forward(transit.at[rows[k]], k, 0, 0).wait_send()
                if where == 2:
                    for n, at in enumerate((1, 0)):
                        forward(w_all.at[slot(at), rows[k]], k, at, n).wait_send()
                if where >= 2:
                    for at in range(4):
                        across(w_in.at[rows[k]], k, at).wait_send()
            if where >= 2:
                keep.wait()

    for i in range(2):

        @pl.when(planes[i] != b)
        def _(leg=legs[i]):
            leg.wait_send()

    for q in range(2):
        copies, here = spread(tok_in, q)
        for copy in copies[1:]:
            copy.wait_send()

        @pl.when(c == q)
        def _(here=here):
            here.wait()

        @pl.when(c != q)
        def _(copy=copies[0]):
            copy.wait_send()

    for i in range(2):
        for j in range(tps):
            if i or j:
                from_e, from_t = (e + i) % 2, (t + j) % tps
                remote(
                    tok_in, tok.at[from_e, from_t], p_send.at[0, 0], p_recv.at[from_e, from_t], partner
                ).wait_recv()


def gather_all(tokens, w, tps):
    chunks = w.shape[0]
    dma = pltpu.SemaphoreType.DMA
    vmem = pl.BlockSpec(memory_space=pltpu.VMEM)
    return pl.pallas_call(
        functools.partial(gather_kernel, tps, chunks),
        out_shape=(
            jax.ShapeDtypeStruct((2, tps) + tokens.shape, BF),
            jax.ShapeDtypeStruct((4,) + w.shape, BF),
        ),
        in_specs=[vmem, vmem],
        out_specs=(vmem, vmem),
        scratch_shapes=[
            pltpu.VMEM((2,) + tokens.shape, BF),
            pltpu.VMEM(w.shape, BF),
            dma((2,)), dma((2,)), dma((2, tps)), dma((2, tps)),
            dma((chunks,)), dma((2, chunks)), dma((4, chunks)), dma((4, chunks)),
            dma((chunks,)), dma((3,)),
        ],
        compiler_params=pltpu.CompilerParams(collective_id=0, has_side_effects=True),
        name="gather_all",
    )(tokens, w)


def attend_kernel(head_size, place_ref, count_ref, q_ref, a_ref, b_ref, c_ref, o_ref, sc, kv_ref):
    tile = pl.program_id(0)

    @pl.when(tile == 0)
    def _():
        many = a_ref.shape[0]
        for n, ref in enumerate((a_ref, b_ref, c_ref)):
            for i in range(many):
                kv_ref[n * many + i] = ref[i]

    tile_len, feats = q_ref.shape
    heads = feats // head_size
    count = count_ref[tile]
    trips = (count + 1) // 2
    inverse = 1.0 / head_size**0.5
    lane = lax.broadcasted_iota(jnp.int32, (tile_len, 2 * tile_len), 1)

    def near(j, first, head):
        cols = slice(first + head * head_size, first + (head + 1) * head_size)
        one = kv_ref[place_ref[tile, 2 * j], :, cols]
        two = kv_ref[place_ref[tile, 2 * j + 1], :, cols]
        return jnp.concatenate([one, two], axis=0)

    def score(j, tops):
        limit = (count - 2 * j) * tile_len
        out = []
        for head in range(heads):
            query = q_ref[:, head * head_size : (head + 1) * head_size]
            scores = lax.dot_general(
                query, near(j, 0, head), (((1,), (1,)), ((), ())), preferred_element_type=F32
            )
            scores = jnp.where(lane < limit, scores * inverse, -1e30)
            sc[j, head] = scores
            out.append(jnp.maximum(tops[head], scores))
        return tuple(out)

    low = jnp.full((tile_len, 2 * tile_len), -1e30, F32)
    tops = lax.fori_loop(0, trips, score, (low,) * heads)
    tops = [jnp.max(top, axis=-1, keepdims=True) for top in tops]

    def weigh(j, sums):
        out = []
        for head in range(heads):
            weights = jnp.exp(sc[j, head] - tops[head])
            sc[j, head] = weights
            out.append(sums[head] + weights)
        return tuple(out)

    sums = lax.fori_loop(0, trips, weigh, (jnp.zeros((tile_len, 2 * tile_len), F32),) * heads)
    shares = [1.0 / jnp.sum(total, axis=-1, keepdims=True) for total in sums]

    def gather(j, totals):
        out = []
        for head in range(heads):
            probs = (sc[j, head] * shares[head]).astype(BF)
            out.append(
                totals[head] + jnp.dot(probs, near(j, feats, head), preferred_element_type=F32)
            )
        return tuple(out)

    totals = lax.fori_loop(0, trips, gather, (jnp.zeros((tile_len, head_size), F32),) * heads)
    for head in range(heads):
        o_ref[:, head * head_size : (head + 1) * head_size] = totals[head].astype(BF)


def attention(place, counts, queries, keys_values, head_size):
    tiles, slots = place.shape
    rows, feats = queries.shape
    tile_len = rows // tiles
    heads = feats // head_size
    many = keys_values[0].shape[0]
    if slots % 2:
        place = jnp.pad(place, ((0, 0), (0, 1)))
    return pl.pallas_call(
        functools.partial(attend_kernel, head_size),
        grid_spec=pltpu.PrefetchScalarGridSpec(
            num_scalar_prefetch=2,
            grid=(tiles,),
            in_specs=[
                pl.BlockSpec((tile_len, feats), lambda i, a, b: (i, 0)),
            ] + [pl.BlockSpec((many, tile_len, 2 * feats), lambda i, a, b: (0, 0, 0))] * 3,
            out_specs=pl.BlockSpec((tile_len, feats), lambda i, a, b: (i, 0)),
            scratch_shapes=[
                pltpu.VMEM(((slots + 1) // 2, heads, tile_len, 2 * tile_len), F32),
                pltpu.VMEM((3 * many, tile_len, 2 * feats), BF),
            ],
        ),
        out_shape=jax.ShapeDtypeStruct((rows, feats), BF),
        cost_estimate=pl.CostEstimate(
            flops=4 * rows * slots * tile_len * feats,
            bytes_accessed=2 * (2 * rows * feats + many * tile_len * 2 * feats),
            transcendentals=rows * slots * tile_len * heads,
        ),
        name="attend",
    )(place, counts, queries, *keys_values)


def finish_kernel(tps, att, w_out, gate, out, joint, core_out, core_in, far_out, far_in, j_send,
                  j_recv, c_send, c_recv, f_send, f_recv, local):
    s, t, b = lax.axis_index("slab"), lax.axis_index("tp"), lax.axis_index("band")
    e, c = s % 2, t % 2
    couples, couple = tps // 2, t // 2
    half = att.shape[2]
    width = out.shape[1]
    other = s + 1 - 2 * e
    alone = (c == b // 2) & (c == b % 2)
    kind = pl.DeviceIdType.MESH

    def dev(slab, tp, band):
        return {"slab": slab, "tp": tp, "band": band}

    to_t, to_b = 2 * couple + b // 2, 2 * (b % 2) + c
    from_t, from_b = 2 * couple + b % 2, 2 * c + b // 2
    partner = dev(s, t + 1 - 2 * c, b)
    across = [dev(s, 2 * ((couple + j) % couples) + c, b) for j in range(1, couples)]
    barrier = pltpu.get_barrier_semaphore()
    peers = [dev(other, to_t, to_b), dev(other, from_t, from_b), partner] + across
    for peer in peers:
        pl.semaphore_signal(barrier, inc=1, device_id=peer, device_id_type=kind)

    @pl.when(jnp.logical_not(alone))
    def _():
        for peer in (dev(s, to_t, to_b), dev(s, from_t, from_b)):
            pl.semaphore_signal(barrier, inc=1, device_id=peer, device_id_type=kind)

    pl.semaphore_wait(barrier, len(peers) + jnp.where(alone, 0, 2))

    def remote(src, dst, send, recv, peer):
        return pltpu.make_async_remote_copy(src, dst, send, recv, device_id=peer, device_id_type=kind)

    away = remote(att.at[1 - e], joint.at[e], j_send.at[1], j_recv.at[e], dev(other, to_t, to_b))
    home = remote(att.at[e], joint.at[e], j_send.at[0], j_recv.at[e], dev(s, to_t, to_b))
    here = pltpu.make_async_copy(att.at[e], joint.at[e], local.at[0])
    away.start()

    @pl.when(alone)
    def _():
        here.start()
        here.wait()

    @pl.when(jnp.logical_not(alone))
    def _():
        home.start()
        home.wait_send()
        home.wait_recv()

    away.wait_send()
    remote(att.at[e], joint.at[1 - e], j_send.at[1], j_recv.at[1 - e], partner).wait_recv()

    def share(j, core):
        target = 2 * ((couple + j) % couples) + core
        cols = pl.ds(pl.multiple_of(target * width, width), width)
        total = jnp.dot(joint[0], w_out[:half, cols], preferred_element_type=F32)
        return total + jnp.dot(joint[1], w_out[half:, cols], preferred_element_type=F32)

    order = list(range(1, couples)) + [0]
    swaps = [
        remote(core_out.at[j], core_in.at[j], c_send.at[j], c_recv.at[j], partner)
        for j in range(couples)
    ]
    sends = [
        remote(far_out.at[j - 1], far_in.at[j - 1], f_send.at[j - 1], f_recv.at[j - 1], across[j - 1])
        for j in range(1, couples)
    ]
    for j in order[:-1]:
        core_out[j] = share(j, 1 - c)
        swaps[j].start()
        mine = share(j, c)
        swaps[j].wait_recv()
        far_out[j - 1] = (mine + core_in[j]).astype(BF)
        sends[j - 1].start()
    core_out[0] = share(0, 1 - c)
    swaps[0].start()
    total = share(0, c)
    swaps[0].wait_recv()
    core_in[0] = total + core_in[0]
    for j in range(1, couples):
        sends[j - 1].wait_recv()
        core_in[0] += far_in[j - 1].astype(F32)
    out[...] = (gate[...] * core_in[0]).astype(BF)
    for j in range(1, couples):
        sends[j - 1].wait_send()
    for j in range(couples):
        swaps[j].wait_send()


def finish(att, w_out, gate, tps):
    rows, half = att.shape[1:]
    width = gate.shape[0]
    couples = tps // 2
    dma = pltpu.SemaphoreType.DMA
    vmem = pl.BlockSpec(memory_space=pltpu.VMEM)
    return pl.pallas_call(
        functools.partial(finish_kernel, tps),
        out_shape=jax.ShapeDtypeStruct((rows, width), BF),
        in_specs=[vmem] * 3,
        out_specs=vmem,
        scratch_shapes=[
            pltpu.VMEM((2, rows, half), BF),
            pltpu.VMEM((couples, rows, width), F32),
            pltpu.VMEM((couples, rows, width), F32),
            pltpu.VMEM((couples - 1, rows, width), BF),
            pltpu.VMEM((couples - 1, rows, width), BF),
            dma((2,)), dma((2,)), dma((couples,)), dma((couples,)),
            dma((couples - 1,)), dma((couples - 1,)), dma((1,)),
        ],
        compiler_params=pltpu.CompilerParams(collective_id=1, has_side_effects=True),
        name="finish",
    )(att, w_out, gate.reshape(1, -1))


def shards(tokens, w_qkv, w_out, shift, scale, gate, q_gain, k_gain, tile_ids, key_counts):
    slabs, bands = lax.axis_size("slab"), lax.axis_size("band")
    slab_pos, band_pos = lax.axis_index("slab"), lax.axis_index("band")
    parity = slab_pos % 2
    tok_rows = tokens.shape[0]
    head_feats = w_out.shape[0]
    half = head_feats // 2
    head_size = q_gain.shape[0]
    tiles = key_counts.shape[0]
    tile_len = tok_rows // tiles
    tps = lax.axis_size("tp")
    tp_pos = lax.axis_index("tp")
    swap = [(i, i ^ 1) for i in range(slabs)]

    band_here = 2 * (band_pos % 2) + tp_pos % 2

    def flat(couple, core, side, low):
        return (2 * couple + core) * bands + 2 * side + low

    every = [
        (couple, i // 4, i // 2 % 2, i % 2) for couple in range(tps // 2) for i in range(8)
    ]
    outward = [(flat(n, c, h, l), flat(n, h, l, c)) for n, c, h, l in every]
    size = tps * bands
    outward_swap = [
        (i * size + source, (i ^ 1) * size + target)
        for i in range(slabs)
        for source, target in outward
    ]
    forward = [
        (flat(n, i % 2, h, i // 2), flat(n, (i + 1) % 2, h, (i + 1) // 2))
        for n in range(tps // 2)
        for h in range(2)
        for i in range(3)
    ]

    def both(ours, theirs, axis):
        return jnp.where(
            parity == 0,
            jnp.concatenate([ours, theirs], axis=axis),
            jnp.concatenate([theirs, ours], axis=axis),
        )

    mine = lax.dynamic_slice_in_dim(w_qkv, parity * half, half, axis=2)
    whole, weights = gather_all(tokens, jnp.stack([mine[:, i] for i in range(3)]), tps)

    lists = jnp.concatenate([tile_ids, key_counts[:, None]], axis=1)
    ours = lax.ppermute(lists, ("tp", "band"), [(b, a) for a, b in outward])
    theirs = lax.ppermute(
        lists, ("slab", "tp", "band"), [(b, a) for a, b in outward_swap]
    )
    lists = both(ours, theirs, 0)
    ids, counts = lists[:, :-1], lists[:, -1]

    joined = project(whole, scale, shift, weights, 1, k_gain, (True, False))
    joined = joined.reshape(2, tiles, tile_len, 2 * half)
    if slabs > 2:
        up = [(i, i + 2) for i in range(slabs - 2)]
        below = lax.ppermute(joined[1], "slab", up)
        above = lax.ppermute(joined[0], "slab", [(b, a) for a, b in up])
        joined = jnp.concatenate([joined, below[None], above[None]], axis=0)
    groups = joined.shape[0]
    left = lax.ppermute(joined, ("tp", "band"), forward)
    right = lax.ppermute(joined, ("tp", "band"), [(b, a) for a, b in forward])
    queries = project(whole, scale, shift, weights, 0, q_gain, (True,))
    near = [part.reshape(groups * tiles, tile_len, 2 * half) for part in (left, joined, right)]

    time_near = ids // (bands * tiles) - (slab_pos - parity)
    group = jnp.where(time_near < 0, 2, jnp.where(time_near > 1, 3, time_near))
    row_near = ids // tiles % bands - band_here + 1
    place = (row_near * groups + group) * tiles + ids % tiles

    attended = attention(place, counts, queries, near, head_size)
    return finish(attended.reshape(2, tok_rows, half), w_out, gate, tps)


def solution(mesh):
    in_specs = (
        P(("slab", "band"), "tp"),
        P("band", None, "tp"),
        P("tp", None),
        P(),
        P(),
        P("tp"),
        P(),
        P(),
        P(("slab", "band"), None),
        P(("slab", "band")),
    )
    out_specs = P(("slab", "band"), "tp")
    return jax.shard_map(shards, mesh=mesh, in_specs=in_specs, out_specs=out_specs, check_vma=False)
```

```python
import functools

import jax
import jax.numpy as jnp
from jax import lax
from jax.experimental import pallas as pl
from jax.experimental.pallas import tpu as pltpu
from jax.sharding import PartitionSpec as P

BF = jnp.bfloat16
F32 = jnp.float32


def proj_kernel(normalize, head_size, x_ref, scale_ref, shift_ref, w_ref, gain_ref, o_ref, normed):
    part = pl.program_id(1)

    @pl.when(part == 0)
    def _():
        floats = jnp.concatenate([x_ref[0, i] for i in range(x_ref.shape[1])], axis=1).astype(F32)
        center = jnp.mean(floats, axis=-1, keepdims=True)
        moved = floats - center
        spread = jnp.mean(moved * moved, axis=-1, keepdims=True)
        normed[...] = (
            moved * lax.rsqrt(spread + 1e-06) * (1.0 + scale_ref[...]) + shift_ref[...]
        ).astype(BF)

    weights = w_ref[...].reshape(normed.shape[1], w_ref.shape[3])
    product = jnp.dot(normed[...], weights, preferred_element_type=F32)

    def write(normed_part):
        for head in range(product.shape[1] // head_size):
            cols = slice(head * head_size, (head + 1) * head_size)
            piece = product[:, cols]
            if normed_part:
                squares = jnp.mean(piece * piece, axis=-1, keepdims=True)
                piece = piece * lax.rsqrt(squares + 1e-06) * gain_ref[...]
            o_ref[:, cols] = piece.astype(BF)

    if all(normalize):
        write(True)
    else:

        @pl.when(part == 0)
        def _():
            write(True)

        @pl.when(part != 0)
        def _():
            write(False)


def project(x, scale, shift, w, first, gain, normalize):
    slabs, pieces, rows, width = x.shape
    width = pieces * width
    parts = len(normalize)
    cols = w.shape[3]
    block = 192 if rows % 192 == 0 else rows
    many = rows // block
    return pl.pallas_call(
        functools.partial(proj_kernel, normalize, gain.shape[0]),
        grid=(slabs * many, parts),
        in_specs=[
            pl.BlockSpec((1, pieces, block, width // pieces), lambda i, j: (i // many, 0, i % many, 0)),
            pl.BlockSpec((1, width), lambda i, j: (0, 0)),
            pl.BlockSpec((1, width), lambda i, j: (0, 0)),
            pl.BlockSpec((w.shape[0], 1) + w.shape[2:], lambda i, j: (0, j + first, 0, 0)),
            pl.BlockSpec((1, gain.shape[0]), lambda i, j: (0, 0)),
        ],
        out_specs=pl.BlockSpec((block, cols), lambda i, j: (i, j)),
        out_shape=jax.ShapeDtypeStruct((slabs * rows, parts * cols), BF),
        scratch_shapes=[pltpu.VMEM((block, width), BF)],
        cost_estimate=pl.CostEstimate(
            flops=2 * slabs * rows * width * parts * cols,
            bytes_accessed=2 * (slabs * rows * width + width * parts * cols),
            transcendentals=0,
        ),
        name="project",
    )(x, scale.reshape(1, -1), shift.reshape(1, -1), w, gain.reshape(1, -1))


def gather_kernel(tps, chunks, tok_in, w_in, tok, w_all, relay, transit, z_send, z_recv, p_send,
                  p_recv, up_send, fwd_send, core_send, w_recv, t_recv, local):
    s, t, b = lax.axis_index("slab"), lax.axis_index("tp"), lax.axis_index("band")
    e, c = s % 2, t % 2
    base = s - e
    couples = tps // 2
    couple = t // 2

    def dev(slab, tp, band):
        return {"slab": slab, "tp": tp, "band": band}

    barrier = pltpu.get_barrier_semaphore()
    peers = [dev(s, t, (b + i) % 4) for i in range(1, 4)]
    for i in range(2):
        for j in range(tps):
            if i or j:
                peers.append(dev(base + (e + i) % 2, (t + j) % tps, b))
    for peer in peers:
        pl.semaphore_signal(barrier, inc=1, device_id=peer, device_id_type=pl.DeviceIdType.MESH)
    pl.semaphore_wait(barrier, len(peers))

    def remote(src, dst, send, recv, peer):
        return pltpu.make_async_remote_copy(
            src, dst, send, recv, device_id=peer, device_id_type=pl.DeviceIdType.MESH
        )

    q_own = b % 2
    planes = [b // 2, 2 + b // 2]
    legs = [
        remote(tok_in, relay.at[q_own], z_send.at[i], z_recv.at[q_own], dev(s, t, planes[i]))
        for i in range(2)
    ]
    for i in range(2):

        @pl.when(planes[i] != b)
        def _(leg=legs[i]):
            leg.start()

    u = jnp.where(c == 1, b, 3 - b)
    step = jnp.where(c == 1, 1, -1)
    ahead, behind = jnp.clip(b + step, 0, 3), jnp.clip(b - step, 0, 3)

    def slot(at):
        return jnp.where(c == 1, at, 3 - at)

    rows = list(range(chunks))
    partner = dev(s, t + 1 - 2 * c, b)

    def own(k, where):
        if where == 0:
            return remote(w_in.at[rows[k]], transit.at[rows[k]], up_send.at[k], t_recv.at[k], dev(s, t, ahead))
        peer = dev(s, t, behind if where == 3 else ahead)
        return remote(w_in.at[rows[k]], w_all.at[b, rows[k]], up_send.at[k], w_recv.at[b, k], peer)

    def forward(src, k, at, n):
        place = slot(at)
        return remote(src, w_all.at[place, rows[k]], fwd_send.at[n, k], w_recv.at[place, k], dev(s, t, ahead))

    def across(src, k, at):
        place = slot(at)
        return remote(src, w_all.at[place, rows[k]], core_send.at[at, k], w_recv.at[place, k], partner)

    def arrived(k, at):
        place = slot(at)
        return remote(w_in.at[rows[k]], w_all.at[place, rows[k]], up_send.at[k], w_recv.at[place, k], partner)

    keep = pltpu.make_async_copy(w_in, w_all.at[b], local.at[2])
    for where in range(4):

        @pl.when(u == where)
        def _(where=where):
            for k in range(chunks):
                own(k, where).start()
            if where >= 2:
                keep.start()
                for k in range(chunks):
                    across(w_in.at[rows[k]], k, where).start()

    def spread(src, q):
        copies = []
        for i in range(2):
            for j in range(couples):
                peer = dev(base + (e + i) % 2, 2 * ((couple + j) % couples) + q, b)
                copies.append(remote(
                    src, tok.at[e, t], p_send.at[q, i * couples + j], p_recv.at[e, t], peer
                ))
        return copies, pltpu.make_async_copy(src, tok.at[e, t], local.at[q])

    for n in range(2):
        q = jnp.where(b < 2, n, 1 - n)
        source = 2 * (b % 2) + q

        def send(src, q=q):
            copies, here = spread(src, q)
            for copy in copies[1:]:
                copy.start()

            @pl.when(c == q)
            def _():
                here.start()

            @pl.when(c != q)
            def _():
                copies[0].start()

        @pl.when(source == b)
        def _(send=send):
            send(tok_in)

        @pl.when(source != b)
        def _(send=send, q=q):
            remote(tok_in, relay.at[q], z_send.at[0], z_recv.at[q], partner).wait_recv()
            send(relay.at[q])

    @pl.when(u == 1)
    def _():
        for k in range(chunks):
            remote(w_in.at[rows[k]], transit.at[rows[k]], up_send.at[k], t_recv.at[k], partner).wait_recv()
            forward(transit.at[rows[k]], k, 0, 0).start()

    @pl.when(u == 2)
    def _():
        for n, at in enumerate((1, 0)):
            for k in range(chunks):
                arrived(k, at).wait_recv()
                src = w_all.at[slot(at), rows[k]]
                forward(src, k, at, n).start()
                across(src, k, at).start()
        for k in range(chunks):
            arrived(k, 3).wait_recv()
            across(w_all.at[slot(3), rows[k]], k, 3).start()

    @pl.when(u == 3)
    def _():
        for at in (2, 1, 0):
            for k in range(chunks):
                arrived(k, at).wait_recv()
                across(w_all.at[slot(at), rows[k]], k, at).start()

    @pl.when(u < 2)
    def _():
        for at in range(4):
            for k in range(chunks):
                arrived(k, at).wait_recv()

    for where in range(4):

        @pl.when(u == where)
        def _(where=where):
            for k in range(chunks):
                own(k, where).wait_send()
                if where == 1:
                    forward(transit.at[rows[k]], k, 0, 0).wait_send()
                if where == 2:
                    for n, at in enumerate((1, 0)):
                        forward(w_all.at[slot(at), rows[k]], k, at, n).wait_send()
                if where >= 2:
                    for at in range(4):
                        across(w_in.at[rows[k]], k, at).wait_send()
            if where >= 2:
                keep.wait()

    for i in range(2):

        @pl.when(planes[i] != b)
        def _(leg=legs[i]):
            leg.wait_send()

    for q in range(2):
        copies, here = spread(tok_in, q)
        for copy in copies[1:]:
            copy.wait_send()

        @pl.when(c == q)
        def _(here=here):
            here.wait()

        @pl.when(c != q)
        def _(copy=copies[0]):
            copy.wait_send()

    for i in range(2):
        for j in range(tps):
            if i or j:
                from_e, from_t = (e + i) % 2, (t + j) % tps
                remote(
                    tok_in, tok.at[from_e, from_t], p_send.at[0, 0], p_recv.at[from_e, from_t], partner
                ).wait_recv()


def gather_all(tokens, w, tps):
    chunks = w.shape[0]
    dma = pltpu.SemaphoreType.DMA
    vmem = pl.BlockSpec(memory_space=pltpu.VMEM)
    return pl.pallas_call(
        functools.partial(gather_kernel, tps, chunks),
        out_shape=(
            jax.ShapeDtypeStruct((2, tps) + tokens.shape, BF),
            jax.ShapeDtypeStruct((4,) + w.shape, BF),
        ),
        in_specs=[vmem, vmem],
        out_specs=(vmem, vmem),
        scratch_shapes=[
            pltpu.VMEM((2,) + tokens.shape, BF),
            pltpu.VMEM(w.shape, BF),
            dma((2,)), dma((2,)), dma((2, tps)), dma((2, tps)),
            dma((chunks,)), dma((2, chunks)), dma((4, chunks)), dma((4, chunks)),
            dma((chunks,)), dma((3,)),
        ],
        compiler_params=pltpu.CompilerParams(collective_id=0, has_side_effects=True),
        name="gather_all",
    )(tokens, w)


def attend_kernel(head_size, place_ref, count_ref, q_ref, a_ref, b_ref, c_ref, o_ref, sc, kv_ref):
    tile = pl.program_id(0)

    @pl.when(tile == 0)
    def _():
        many = a_ref.shape[0]
        for n, ref in enumerate((a_ref, b_ref, c_ref)):
            for i in range(many):
                kv_ref[n * many + i] = ref[i]

    tile_len, feats = q_ref.shape
    heads = feats // head_size
    count = count_ref[tile]
    trips = (count + 1) // 2
    inverse = 1.0 / head_size**0.5
    lane = lax.broadcasted_iota(jnp.int32, (tile_len, 2 * tile_len), 1)

    def near(j, first, head):
        cols = slice(first + head * head_size, first + (head + 1) * head_size)
        one = kv_ref[place_ref[tile, 2 * j], :, cols]
        two = kv_ref[place_ref[tile, 2 * j + 1], :, cols]
        return jnp.concatenate([one, two], axis=0)

    def score(j, tops):
        limit = (count - 2 * j) * tile_len
        out = []
        for head in range(heads):
            query = q_ref[:, head * head_size : (head + 1) * head_size]
            scores = lax.dot_general(
                query, near(j, 0, head), (((1,), (1,)), ((), ())), preferred_element_type=F32
            )
            scores = jnp.where(lane < limit, scores * inverse, -1e30)
            sc[j, head] = scores
            out.append(jnp.maximum(tops[head], scores))
        return tuple(out)

    low = jnp.full((tile_len, 2 * tile_len), -1e30, F32)
    tops = lax.fori_loop(0, trips, score, (low,) * heads)
    tops = [jnp.max(top, axis=-1, keepdims=True) for top in tops]

    def weigh(j, sums):
        out = []
        for head in range(heads):
            weights = jnp.exp(sc[j, head] - tops[head])
            sc[j, head] = weights
            out.append(sums[head] + weights)
        return tuple(out)

    sums = lax.fori_loop(0, trips, weigh, (jnp.zeros((tile_len, 2 * tile_len), F32),) * heads)
    shares = [1.0 / jnp.sum(total, axis=-1, keepdims=True) for total in sums]

    def gather(j, totals):
        out = []
        for head in range(heads):
            probs = (sc[j, head] * shares[head]).astype(BF)
            out.append(
                totals[head] + jnp.dot(probs, near(j, feats, head), preferred_element_type=F32)
            )
        return tuple(out)

    totals = lax.fori_loop(0, trips, gather, (jnp.zeros((tile_len, head_size), F32),) * heads)
    for head in range(heads):
        o_ref[:, head * head_size : (head + 1) * head_size] = totals[head].astype(BF)


def attention(place, counts, queries, keys_values, head_size):
    tiles, slots = place.shape
    rows, feats = queries.shape
    tile_len = rows // tiles
    heads = feats // head_size
    many = keys_values[0].shape[0]
    if slots % 2:
        place = jnp.pad(place, ((0, 0), (0, 1)))
    return pl.pallas_call(
        functools.partial(attend_kernel, head_size),
        grid_spec=pltpu.PrefetchScalarGridSpec(
            num_scalar_prefetch=2,
            grid=(tiles,),
            in_specs=[
                pl.BlockSpec((tile_len, feats), lambda i, a, b: (i, 0)),
            ] + [pl.BlockSpec((many, tile_len, 2 * feats), lambda i, a, b: (0, 0, 0))] * 3,
            out_specs=pl.BlockSpec((tile_len, feats), lambda i, a, b: (i, 0)),
            scratch_shapes=[
                pltpu.VMEM(((slots + 1) // 2, heads, tile_len, 2 * tile_len), F32),
                pltpu.VMEM((3 * many, tile_len, 2 * feats), BF),
            ],
        ),
        out_shape=jax.ShapeDtypeStruct((rows, feats), BF),
        cost_estimate=pl.CostEstimate(
            flops=4 * rows * slots * tile_len * feats,
            bytes_accessed=2 * (2 * rows * feats + many * tile_len * 2 * feats),
            transcendentals=rows * slots * tile_len * heads,
        ),
        name="attend",
    )(place, counts, queries, *keys_values)


def finish_kernel(tps, att, w_out, gate, out, joint, core_out, core_in, far_out, far_in, j_send,
                  j_recv, c_send, c_recv, f_send, f_recv, local):
    s, t, b = lax.axis_index("slab"), lax.axis_index("tp"), lax.axis_index("band")
    e, c = s % 2, t % 2
    couples, couple = tps // 2, t // 2
    half = att.shape[2]
    width = out.shape[1]
    other = s + 1 - 2 * e
    alone = (c == b // 2) & (c == b % 2)
    kind = pl.DeviceIdType.MESH

    def dev(slab, tp, band):
        return {"slab": slab, "tp": tp, "band": band}

    to_t, to_b = 2 * couple + b // 2, 2 * (b % 2) + c
    from_t, from_b = 2 * couple + b % 2, 2 * c + b // 2
    partner = dev(s, t + 1 - 2 * c, b)
    across = [dev(s, 2 * ((couple + j) % couples) + c, b) for j in range(1, couples)]
    barrier = pltpu.get_barrier_semaphore()
    peers = [dev(other, to_t, to_b), dev(other, from_t, from_b), partner] + across
    for peer in peers:
        pl.semaphore_signal(barrier, inc=1, device_id=peer, device_id_type=kind)

    @pl.when(jnp.logical_not(alone))
    def _():
        for peer in (dev(s, to_t, to_b), dev(s, from_t, from_b)):
            pl.semaphore_signal(barrier, inc=1, device_id=peer, device_id_type=kind)

    pl.semaphore_wait(barrier, len(peers) + jnp.where(alone, 0, 2))

    def remote(src, dst, send, recv, peer):
        return pltpu.make_async_remote_copy(src, dst, send, recv, device_id=peer, device_id_type=kind)

    away = remote(att.at[1 - e], joint.at[e], j_send.at[1], j_recv.at[e], dev(other, to_t, to_b))
    home = remote(att.at[e], joint.at[e], j_send.at[0], j_recv.at[e], dev(s, to_t, to_b))
    here = pltpu.make_async_copy(att.at[e], joint.at[e], local.at[0])
    away.start()

    @pl.when(alone)
    def _():
        here.start()
        here.wait()

    @pl.when(jnp.logical_not(alone))
    def _():
        home.start()
        home.wait_send()
        home.wait_recv()

    away.wait_send()
    remote(att.at[e], joint.at[1 - e], j_send.at[1], j_recv.at[1 - e], partner).wait_recv()

    def share(j, core):
        target = 2 * ((couple + j) % couples) + core
        cols = pl.ds(pl.multiple_of(target * width, width), width)
        total = jnp.dot(joint[0], w_out[:half, cols], preferred_element_type=F32)
        return total + jnp.dot(joint[1], w_out[half:, cols], preferred_element_type=F32)

    order = list(range(1, couples)) + [0]
    swaps = [
        remote(core_out.at[j], core_in.at[j], c_send.at[j], c_recv.at[j], partner)
        for j in range(couples)
    ]
    sends = [
        remote(far_out.at[j - 1], far_in.at[j - 1], f_send.at[j - 1], f_recv.at[j - 1], across[j - 1])
        for j in range(1, couples)
    ]
    for j in order[:-1]:
        core_out[j] = share(j, 1 - c)
        swaps[j].start()
        mine = share(j, c)
        swaps[j].wait_recv()
        far_out[j - 1] = (mine + core_in[j]).astype(BF)
        sends[j - 1].start()
    core_out[0] = share(0, 1 - c)
    swaps[0].start()
    total = share(0, c)
    swaps[0].wait_recv()
    core_in[0] = total + core_in[0]
    for j in range(1, couples):
        sends[j - 1].wait_recv()
        core_in[0] += far_in[j - 1].astype(F32)
    out[...] = (gate[...] * core_in[0]).astype(BF)
    for j in range(1, couples):
        sends[j - 1].wait_send()
    for j in range(couples):
        swaps[j].wait_send()


def finish(att, w_out, gate, tps):
    rows, half = att.shape[1:]
    width = gate.shape[0]
    couples = tps // 2
    dma = pltpu.SemaphoreType.DMA
    vmem = pl.BlockSpec(memory_space=pltpu.VMEM)
    return pl.pallas_call(
        functools.partial(finish_kernel, tps),
        out_shape=jax.ShapeDtypeStruct((rows, width), BF),
        in_specs=[vmem] * 3,
        out_specs=vmem,
        scratch_shapes=[
            pltpu.VMEM((2, rows, half), BF),
            pltpu.VMEM((couples, rows, width), F32),
            pltpu.VMEM((couples, rows, width), F32),
            pltpu.VMEM((couples - 1, rows, width), BF),
            pltpu.VMEM((couples - 1, rows, width), BF),
            dma((2,)), dma((2,)), dma((couples,)), dma((couples,)),
            dma((couples - 1,)), dma((couples - 1,)), dma((1,)),
        ],
        compiler_params=pltpu.CompilerParams(collective_id=1, has_side_effects=True),
        name="finish",
    )(att, w_out, gate.reshape(1, -1))


def shards(tokens, w_qkv, w_out, shift, scale, gate, q_gain, k_gain, tile_ids, key_counts):
    slabs, bands = lax.axis_size("slab"), lax.axis_size("band")
    slab_pos, band_pos = lax.axis_index("slab"), lax.axis_index("band")
    parity = slab_pos % 2
    tok_rows = tokens.shape[0]
    head_feats = w_out.shape[0]
    half = head_feats // 2
    head_size = q_gain.shape[0]
    tiles = key_counts.shape[0]
    tile_len = tok_rows // tiles
    tps = lax.axis_size("tp")
    tp_pos = lax.axis_index("tp")
    swap = [(i, i ^ 1) for i in range(slabs)]

    band_here = 2 * (band_pos % 2) + tp_pos % 2

    def flat(couple, core, side, low):
        return (2 * couple + core) * bands + 2 * side + low

    every = [
        (couple, i // 4, i // 2 % 2, i % 2) for couple in range(tps // 2) for i in range(8)
    ]
    outward = [(flat(n, c, h, l), flat(n, h, l, c)) for n, c, h, l in every]
    size = tps * bands
    outward_swap = [
        (i * size + source, (i ^ 1) * size + target)
        for i in range(slabs)
        for source, target in outward
    ]
    forward = [
        (flat(n, i % 2, h, i // 2), flat(n, (i + 1) % 2, h, (i + 1) // 2))
        for n in range(tps // 2)
        for h in range(2)
        for i in range(3)
    ]

    def both(ours, theirs, axis):
        return jnp.where(
            parity == 0,
            jnp.concatenate([ours, theirs], axis=axis),
            jnp.concatenate([theirs, ours], axis=axis),
        )

    mine = lax.dynamic_slice_in_dim(w_qkv, parity * half, half, axis=2)
    whole, weights = gather_all(tokens, jnp.stack([mine[:, i] for i in range(3)]), tps)

    lists = jnp.concatenate([tile_ids, key_counts[:, None]], axis=1)
    ours = lax.ppermute(lists, ("tp", "band"), [(b, a) for a, b in outward])
    theirs = lax.ppermute(
        lists, ("slab", "tp", "band"), [(b, a) for a, b in outward_swap]
    )
    lists = both(ours, theirs, 0)
    ids, counts = lists[:, :-1], lists[:, -1]

    joined = project(whole, scale, shift, weights, 1, k_gain, (True, False))
    joined = joined.reshape(2, tiles, tile_len, 2 * half)
    if slabs > 2:
        up = [(i, i + 2) for i in range(slabs - 2)]
        below = lax.ppermute(joined[1], "slab", up)
        above = lax.ppermute(joined[0], "slab", [(b, a) for a, b in up])
        joined = jnp.concatenate([joined, below[None], above[None]], axis=0)
    groups = joined.shape[0]
    left = lax.ppermute(joined, ("tp", "band"), forward)
    right = lax.ppermute(joined, ("tp", "band"), [(b, a) for a, b in forward])
    queries = project(whole, scale, shift, weights, 0, q_gain, (True,))
    near = [part.reshape(groups * tiles, tile_len, 2 * half) for part in (left, joined, right)]

    time_near = ids // (bands * tiles) - (slab_pos - parity)
    group = jnp.where(time_near < 0, 2, jnp.where(time_near > 1, 3, time_near))
    row_near = ids // tiles % bands - band_here + 1
    place = (row_near * groups + group) * tiles + ids % tiles

    attended = attention(place, counts, queries, near, head_size)
    return finish(attended.reshape(2, tok_rows, half), w_out, gate, tps)


def solution(mesh):
    in_specs = (
        P(("slab", "band"), "tp"),
        P("band", None, "tp"),
        P("tp", None),
        P(),
        P(),
        P("tp"),
        P(),
        P(),
        P(("slab", "band"), None),
        P(("slab", "band")),
    )
    out_specs = P(("slab", "band"), "tp")
    return jax.shard_map(shards, mesh=mesh, in_specs=in_specs, out_specs=out_specs, check_vma=False)
```
